32 devices in a mesh: row: 8 (over z, y), col: 4 (over x, core).
Axes of the slice: x: 2, y: 2, z: 4, core: 2. Of those that a mesh axis runs over, the one named last changes fastest.
Arguments:
- tensor: bfloat16 [1024, 64, 512], P('row', None, 'col'), may hold values from -6 to 6
- loss_kind: int32 [1024, 64, 512], P('row', None, 'col'), may hold values from 0 to 1, as said below
- factor_one: float32 [1024, 512], P(('row', 'col')), may hold values from -2 to 2
- factor_two: float32 [512, 512], P(('col', 'row')), may hold values from -2 to 2
- factor_three: float32 [64, 512], replicated, may hold values from -2 to 2
- first_one: float32 [1024, 512], P(('row', 'col')), may hold values from -0.03 to 0.03
- second_one: float32 [1024, 512], P(('row', 'col')), may hold values from 0.0005 to 0.05
- first_two: float32 [512, 512], P(('col', 'row')), may hold values from -0.03 to 0.03
- second_two: float32 [512, 512], P(('col', 'row')), may hold values from 0.0005 to 0.05
- first_three: float32 [64, 512], replicated, may hold values from -0.03 to 0.03
- second_three: float32 [64, 512], replicated, may hold values from 0.0005 to 0.05
Outputs:
- new_one: float32 [1024, 512], P(('row', 'col'))
- new_two: float32 [512, 512], P(('col', 'row'))
- new_three: float32 [64, 512], replicated
The draws below stay inside these ranges and needn't reach their ends.
Inputs may be any that keep to these rules, and one draw needn't show every extreme that they name: loss_kind takes one value on each block of 128 first-mode by 128 second-mode indices (with all 64 third-mode ones), aligned to multiples of 128 and 128, and is 1 on exactly half of these blocks.
All inputs are finite; a program needn't handle non-finite values.
Results may differ from the reference program's by a relative error of at most 0.003.
Values may be sent and summed in bfloat16 or wider, within the bound.
A program may use at most 128 MiB of HBM per device.

```python
import math
import jax
import jax.numpy as jnp
from jax import lax

TI = 128
TJ = 128
K = 64
R = 512
ITERS = 2
STEP = 10
I = 1024
J = 512
N_ROW = 8


def draw_tensor(key, part):
    key_offset, key_gain, key_noise = jax.random.split(key, 3)
    row_blocks = I // TI
    col_blocks = J // TJ
    block_shape = (row_blocks, 1, 1, col_blocks, 1)
    full_shape = (row_blocks, TI, K, col_blocks, TJ)
    offset = jax.random.uniform(key_offset, block_shape, jnp.float32, -1.0, 1.0)
    gain = jnp.exp(jax.random.uniform(key_gain, block_shape, jnp.float32, -1.5, 0.7))
    noise = jax.random.normal(key_noise, full_shape, jnp.float32)
    values = jnp.clip(offset + gain * noise, -6.0, 6.0)
    return values.reshape(I, K, J).astype(jnp.bfloat16)


def draw_loss_kind(key, part):
    row_blocks = I // TI
    col_blocks = J // TJ
    order = jax.random.permutation(key, row_blocks * col_blocks)
    block_kind = (order % 2).astype(jnp.int32).reshape(row_blocks, 1, 1, col_blocks, 1)
    return jnp.broadcast_to(block_kind, (row_blocks, TI, K, col_blocks, TJ)).reshape(I, K, J)


def shard_levels(key, shape, pieces, smallest, high):
    factor_of = 1.0
    for dim, blocks in pieces:
        heights = jax.random.uniform(jax.random.fold_in(jax.random.fold_in(key, 6), dim), (blocks,), jnp.float32, smallest / len(pieces), high / len(pieces))
        factor_of = factor_of * jnp.repeat(jnp.exp(heights), shape[dim] // blocks).reshape((-1,) + (1,) * (len(shape) - 1 - dim))
    return factor_of


def bell_draw(rng, dims, deviation, most, cuts=(), held_as=jnp.bfloat16):
    level = shard_levels(rng, dims, cuts, -0.22, 0.18) if cuts else 1.0
    drawn = jax.random.normal(rng, dims, jnp.float32) * deviation * level
    return jnp.minimum(jnp.maximum(drawn, -most), most).astype(held_as)


def setup_inputs(seed: int = 0) -> dict:
    seeds = jax.random.split(jax.random.key(seed), 12)
    tensor = draw_tensor(jax.random.fold_in(seeds[11], 71), 0)
    loss_kind = draw_loss_kind(jax.random.fold_in(seeds[11], 71), 0)
    factor_one = bell_draw(seeds[2], (I, R), 0.35, 2.0, ((0, 32),), jnp.float32)
    factor_two = bell_draw(seeds[3], (J, R), 0.35, 2.0, ((0, 32),), jnp.float32)
    factor_three = bell_draw(seeds[4], (K, R), 0.35, 2.0, (), jnp.float32)
    first_one = bell_draw(seeds[5], (I, R), 0.005, 0.03, ((0, 32),), jnp.float32)
    second_one = jnp.clip(jnp.exp(math.log(0.05) - 4.6051702 * jax.random.uniform(seeds[6], (I, R), jnp.float32) ** shard_levels(seeds[6], (I, R), ((0, 32),), -0.2, 0.2)), 0.0005, 0.05)
    first_two = bell_draw(seeds[7], (J, R), 0.005, 0.03, ((0, 32),), jnp.float32)
    second_two = jnp.clip(jnp.exp(math.log(0.05) - 4.6051702 * jax.random.uniform(seeds[8], (J, R), jnp.float32) ** shard_levels(seeds[8], (J, R), ((0, 32),), -0.2, 0.2)), 0.0005, 0.05)
    first_three = bell_draw(seeds[9], (K, R), 0.005, 0.03, (), jnp.float32)
    second_three = jnp.clip(jnp.exp(jax.random.uniform(seeds[10], (K, R), jnp.float32, math.log(0.0005), math.log(0.05))), 0.0005, 0.05)
    return dict(tensor=tensor, loss_kind=loss_kind, factor_one=factor_one, factor_two=factor_two, factor_three=factor_three, first_one=first_one, second_one=second_one, first_two=first_two, second_two=second_two, first_three=first_three, second_three=second_three)


learn_rate = 0.05
beta_one = 0.8
beta_two = 0.95
adam_eps = 1e-08

def loss_slope(rebuilt, values, kinds):
    excess = rebuilt - values
    huber_part = jnp.clip(excess, -1.0, 1.0)
    target = jnp.where(values > 0, 1.0, 0.0).astype(rebuilt.dtype)
    logit_part = jax.nn.sigmoid(rebuilt) - target
    return jnp.where(kinds == 1, logit_part, huber_part)

def adam_step(param, first, second, grad, counter):
    first = beta_one * first + (1.0 - beta_one) * grad
    second = beta_two * second + (1.0 - beta_two) * grad * grad
    corr_one = 1.0 - beta_one ** counter
    corr_two = 1.0 - beta_two ** counter
    param = param - learn_rate * (first / corr_one) / (jnp.sqrt(second / corr_two) + adam_eps)
    return (param, first, second)

def all_grads(tensor, loss_kind, half_one, half_two, half_three):
    three_f = half_three.astype(jnp.float32)
    blocks = (tensor.reshape(N_ROW, TI, K, J), loss_kind.reshape(N_ROW, TI, K, J), half_one.reshape(N_ROW, TI, R))

    def block_step(carry, items):
        grad_two, grad_three = carry
        data_blk, kind_blk, one_blk = items
        one_f = one_blk.astype(jnp.float32)
        scaled_rows = (one_f[:, None, :] * three_f[None, :, :]).astype(jnp.bfloat16).reshape(TI * K, R)
        rebuilt = lax.dot_general(scaled_rows, half_two, (((1,), (1,)), ((), ())), preferred_element_type=jnp.float32)
        values = data_blk.reshape(TI * K, J).astype(jnp.float32)
        deriv_bf = loss_slope(rebuilt, values, kind_blk.reshape(TI * K, J)).astype(jnp.bfloat16)
        projected = jnp.dot(deriv_bf, half_two, preferred_element_type=jnp.float32).reshape(TI, K, R)
        grad_one = lax.optimization_barrier(jnp.sum(projected * three_f[None, :, :], axis=1))
        grad_three = grad_three + lax.optimization_barrier(jnp.sum(projected * one_f[:, None, :], axis=0))
        grad_two = grad_two + lax.dot_general(deriv_bf, scaled_rows, (((0,), (0,)), ((), ())), preferred_element_type=jnp.float32)
        return ((grad_two, grad_three), grad_one)
    start = (jnp.zeros((J, R), jnp.float32), jnp.zeros((K, R), jnp.float32))
    (grad_two, grad_three), grad_one = lax.scan(block_step, start, blocks)
    grad_one = grad_one.reshape(I, R) / math.sqrt(J * K)
    grad_two = grad_two / math.sqrt(I * K)
    grad_three = grad_three / math.sqrt(I * J)
    return (grad_one, grad_two, grad_three)

def reference(tensor, loss_kind, factor_one, factor_two, factor_three, first_one, second_one, first_two, second_two, first_three, second_three):
    start_one, start_two, start_three = (factor_one, factor_two, factor_three)
    for iteration in range(ITERS):
        grad_one, grad_two, grad_three = all_grads(tensor, loss_kind, factor_one.astype(jnp.bfloat16), factor_two.astype(jnp.bfloat16), factor_three.astype(jnp.bfloat16))
        counter = STEP + iteration + 1
        factor_one, first_one, second_one = adam_step(factor_one, first_one, second_one, grad_one, counter)
        factor_two, first_two, second_two = adam_step(factor_two, first_two, second_two, grad_two, counter)
        factor_three, first_three, second_three = adam_step(factor_three, first_three, second_three, grad_three, counter)
    spread = learn_rate * ITERS
    return ((start_one - factor_one) / spread, (start_two - factor_two) / spread, (start_three - factor_three) / spread)
```

```python
import functools
import math

import jax
import jax.numpy as jnp
from jax import lax
from jax.experimental import pallas as pl
from jax.experimental.pallas import tpu as pltpu
from jax.sharding import PartitionSpec as P

ITERS = 2
STEP = 10
HALVES = 2
P_ROWS = 16
Z_ROWS = 64
LANES = 128

learn_rate = 0.05
beta_one = 0.8
beta_two = 0.95
adam_eps = 1e-08

F32 = jnp.float32
BF16 = jnp.bfloat16


def adam_step(param, first, second, grad, counter):
    first = beta_one * first + (1.0 - beta_one) * grad
    second = beta_two * second + (1.0 - beta_two) * grad * grad
    corr_one = 1.0 - beta_one**counter
    corr_two = 1.0 - beta_two**counter
    param = param - learn_rate * (first / corr_one) / (jnp.sqrt(second / corr_two) + adam_eps)
    return (param, first, second)


def kernel(
    n_row, n_col, scales,
    tensor, kind, a_hbm, b_hbm, c_hbm, ma_hbm, va_hbm, mb_hbm, vb_hbm, mc_hbm, vc_hbm,
    oa, ob, oc,
    x_s, kind_s, ag_a, ag_b, ag_bh, ag_c, gs_a, gs_b, gs_c, rs_a, rs_b, rs_c,
    a_b, a_f, c_b, c_f, ga, gb, gc, st_a, st_b, st_c, split, p_s, y_s, m_s, out_a, out_b, out_c,
    a_in, b_in, c_in, ma_in, va_in, mb_in, vb_in, mc_in, vc_in,
    load_sem, sends, recvs, out_sem,
):
    row = lax.axis_index("row")
    col = lax.axis_index("col")
    n_all = n_row * n_col
    me = row * n_col + col
    tile_rows, depth, tile_cols = x_s.shape
    rank = a_f.shape[1]
    half = rank // HALVES
    own_a = a_in.shape[0]
    own_b = b_in.shape[0]
    chunk = st_c.shape[1]
    groups = rank // LANES

    load_x = pltpu.make_async_copy(tensor, x_s, load_sem.at[0])
    load_k = pltpu.make_async_copy(kind.at[0, pl.ds(0, 8)], kind_s, load_sem.at[1])

    pairs = (
        (a_hbm, a_in), (b_hbm, b_in), (c_hbm, c_in), (ma_hbm, ma_in), (va_hbm, va_in),
        (mb_hbm, mb_in), (vb_hbm, vb_in), (mc_hbm, mc_in), (vc_hbm, vc_in),
    )
    loads = [
        pltpu.make_async_copy(src, dst, load_sem.at[2 + i]) for i, (src, dst) in enumerate(pairs)
    ]

    def device(d):
        return {"row": lax.div(d, n_col), "col": lax.rem(d, n_col)}

    kinds = {
        "a": (n_col, col, lambda d: {"col": d}),
        "b": (n_row, row, lambda d: {"row": d}),
        "c": (n_all, me, device),
    }
    barrier = pltpu.get_barrier_semaphore()

    for what in "ba":
        n, mine, target = kinds[what]

        def greet(k, carry):
            pl.semaphore_signal(
                barrier, inc=1, device_id=target(lax.rem(mine + k, n)),
                device_id_type=pl.DeviceIdType.MESH,
            )
            return carry

        lax.fori_loop(1, n, greet, 0)

    for load in loads:
        load.start()
    load_k.start()
    load_x.start()

    slots = {}

    def copy(src, dst, what, slot, target):
        return pltpu.make_async_remote_copy(
            src_ref=src, dst_ref=dst, send_sem=sends.at[slot], recv_sem=recvs.at[slot],
            device_id=kinds[what][2](target), device_id_type=pl.DeviceIdType.MESH,
        )

    def start(what, key, scatter, src, dst):
        slot = slots[what, key, scatter] = len(slots)
        n, mine, _ = kinds[what]

        def body(k, carry):
            peer = lax.rem(mine + k, n)
            copy(src.at[peer if scatter else mine], dst.at[mine], what, slot, peer).start()
            return carry

        lax.fori_loop(1, n, body, 0)
        started.append((what, key, scatter, src, dst))

    def whole(what, key, scatter, src, dst):
        n, mine, _ = kinds[what]
        part = pl.ds(0, n - 1)
        return copy(
            src.at[part], dst.at[part], what, slots[what, key, scatter], lax.rem(mine + 1, n)
        )

    started = []

    for load in loads[:3]:
        load.wait()
    a = a_in[...]
    b = b_in[...]
    ag_a[0, col] = a.astype(BF16)
    ag_b[row] = b.astype(BF16)

    pl.semaphore_wait(barrier, n_row + n_col - 2)
    start("b", 0, False, ag_b, ag_b)
    start("a", 0, False, ag_a.at[0], ag_a.at[0])

    for load in loads[3:]:
        load.wait()
    for i, ref in enumerate((c_in, mc_in, vc_in)):
        for d in range(n_all):
            g, h = d // groups, d % groups
            split[i, d] = ref[g * chunk : (g + 1) * chunk, h * LANES : (h + 1) * LANES]
    st_a[0], st_a[1], st_a[2] = a, ma_in[...], va_in[...]
    st_b[0], st_b[1], st_b[2] = b, mb_in[...], vb_in[...]
    st_c[0], st_c[1], st_c[2] = split[0, me], split[1, me], split[2, me]
    c_b[...] = c_in[...].astype(BF16)
    load_x.wait()
    load_k.wait()

    def act(m):
        x = x_s[...].reshape(tile_rows * depth, tile_cols).astype(F32)
        huber = jnp.clip(m - x, -1.0, 1.0)
        logit = 0.5 * jnp.tanh(0.5 * m) + jnp.where(x > 0, -0.5, 0.5)
        is_logit = jnp.broadcast_to(kind_s[0:1, :], m.shape) == 1
        y_s[...] = jnp.where(is_logit, logit, huber).astype(BF16)

    def product(p, b):
        return lax.dot_general(p, b, (((1,), (1,)), ((), ())), preferred_element_type=F32)

    spread = learn_rate * ITERS
    for it in range(ITERS):
        last = it == ITERS - 1
        counter = STEP + it + 1

        whole("a", it, False, ag_a.at[it], ag_a.at[it]).wait_recv()
        a_b[...] = ag_a[it].reshape(tile_rows, rank)
        a_f[...] = a_b[...].astype(F32)
        if it > 0:
            whole("c", it, False, ag_c.at[it], ag_c.at[it]).wait_recv()
            for d in range(n_all):
                g, h = d // groups, d % groups
                c_b[g * chunk : (g + 1) * chunk, h * LANES : (h + 1) * LANES] = ag_c[it, d]
        c_f[...] = c_b[...].astype(F32)

        def scale_rows(s, carry):
            at = pl.ds(pl.multiple_of(s * P_ROWS, P_ROWS), P_ROWS)
            span = pl.ds(pl.multiple_of(s * P_ROWS * depth, P_ROWS * depth), P_ROWS * depth)
            p = a_b[at, :][:, None, :] * c_b[...][None]
            p_s[span, :] = p.reshape(P_ROWS * depth, rank)
            return carry

        lax.fori_loop(0, tile_rows // P_ROWS, scale_rows, 0)

        if it == 0:
            whole("b", 0, False, ag_b, ag_b).wait_recv()
            bh = ag_b[...].reshape(tile_cols, rank)
            act(product(p_s[...], bh))
        else:
            for h in range(HALVES):
                whole("b", (it, h), False, ag_bh.at[it, h], ag_bh.at[it, h]).wait_recv()
                m = product(
                    p_s[:, h * half : (h + 1) * half], ag_bh[it, h].reshape(tile_cols, half)
                )
                if h > 0:
                    m = m_s[...] + m
                if h < HALVES - 1:
                    m_s[...] = m
                else:
                    act(m)
            bh = jnp.concatenate(
                [ag_bh[it, h].reshape(tile_cols, half) for h in range(HALVES)], axis=1
            )

        gc[...] = jnp.zeros_like(gc)

        def project(s, carry):
            at = pl.ds(pl.multiple_of(s * Z_ROWS, Z_ROWS), Z_ROWS)
            span = pl.ds(pl.multiple_of(s * Z_ROWS * depth, Z_ROWS * depth), Z_ROWS * depth)
            z = jnp.dot(y_s[span, :], bh, preferred_element_type=F32)
            z = z.reshape(Z_ROWS, depth, rank)
            ga[at, :] = jnp.sum(z * c_f[...][None], axis=1) * scales[0]
            gc[...] += jnp.sum(z * a_f[at, :][:, None, :], axis=0)
            return carry

        lax.fori_loop(0, tile_rows // Z_ROWS, project, 0)

        for d in range(n_all):
            g, h = d // groups, d % groups
            gs_c[it, d] = (
                gc[g * chunk : (g + 1) * chunk, h * LANES : (h + 1) * LANES] * scales[2]
            ).astype(BF16)
        start("c", it, True, gs_c.at[it], rs_c.at[it])
        rs_c[it, me] = gs_c[it, me]
        gs_a[it] = ga[...].astype(BF16).reshape(n_col, own_a, rank)
        start("a", it, True, gs_a.at[it], rs_a.at[it])

        for h in range(HALVES):
            cut = slice(h * half, (h + 1) * half)
            g = lax.dot_general(
                y_s[...], p_s[:, cut], (((0,), (0,)), ((), ())), preferred_element_type=F32
            ) * scales[1]
            gb[:, cut] = g
            gs_b[it, h] = g.astype(BF16).reshape(n_row, own_b, half)
            start("b", (it, h), True, gs_b.at[it, h], rs_b.at[it, h])

        whole("a", it, True, gs_a.at[it], rs_a.at[it]).wait_recv()
        grad = ga[pl.ds(pl.multiple_of(col * own_a, own_a), own_a), :]
        for k in range(1, n_col):
            grad = grad + rs_a[it, lax.rem(col + k, n_col)].astype(F32)
        st_a[0], st_a[1], st_a[2] = adam_step(st_a[0], st_a[1], st_a[2], grad, counter)
        if last:
            out_a[...] = (a_in[...] - st_a[0]) / spread
            put_a = pltpu.make_async_copy(out_a, oa, out_sem.at[0])
            put_a.start()
        else:
            ag_a[it + 1, col] = st_a[0].astype(BF16)
            start("a", it + 1, False, ag_a.at[it + 1], ag_a.at[it + 1])

        whole("c", it, True, gs_c.at[it], rs_c.at[it]).wait_recv()
        st_c[0], st_c[1], st_c[2] = adam_step(
            st_c[0], st_c[1], st_c[2], jnp.sum(rs_c[it].astype(F32), axis=0), counter
        )
        c = (split[0, me] - st_c[0]) / spread if last else st_c[0]
        ag_c[it + 1, me] = c.astype(BF16)
        start("c", it + 1, False, ag_c.at[it + 1], ag_c.at[it + 1])

        for h in range(HALVES):
            cut = slice(h * half, (h + 1) * half)
            whole("b", (it, h), True, gs_b.at[it, h], rs_b.at[it, h]).wait_recv()
            grad = gb[pl.ds(pl.multiple_of(row * own_b, own_b), own_b), cut]
            for k in range(1, n_row):
                grad = grad + rs_b[it, h, lax.rem(row + k, n_row)].astype(F32)
            f, m, v = adam_step(st_b[0, :, cut], st_b[1, :, cut], st_b[2, :, cut], grad, counter)
            if last:
                out_b[:, cut] = (b_in[:, cut] - f) / spread
            else:
                st_b[0, :, cut], st_b[1, :, cut], st_b[2, :, cut] = f, m, v
                ag_bh[it + 1, h, row] = f.astype(BF16)
                start("b", (it + 1, h), False, ag_bh.at[it + 1, h], ag_bh.at[it + 1, h])
        if last:
            put_b = pltpu.make_async_copy(out_b, ob, out_sem.at[1])
            put_b.start()

    whole("c", ITERS, False, ag_c.at[ITERS], ag_c.at[ITERS]).wait_recv()
    for d in range(n_all):
        g, h = d // groups, d % groups
        out_c[g * chunk : (g + 1) * chunk, h * LANES : (h + 1) * LANES] = ag_c[ITERS, d].astype(F32)
    put_c = pltpu.make_async_copy(out_c, oc, out_sem.at[2])
    put_c.start()
    for args in started:
        whole(*args).wait_send()
    for put in (put_a, put_b, put_c):
        put.wait()


def hand_on(a, b, c, oa, ob, oc, sems):
    moves = [
        pltpu.make_async_copy(src, dst, sems.at[i])
        for i, (src, dst) in enumerate(((a, oa), (b, ob), (c, oc)))
    ]
    for move in moves:
        move.start()
    for move in moves:
        move.wait()


def shards(tensor, loss_kind, a, b, c, ma, va, mb, vb, mc, vc):
    tile_rows, depth, tile_cols = tensor.shape
    rank = a.shape[1]
    half = rank // HALVES
    n_row = lax.axis_size("row")
    n_col = lax.axis_size("col")
    n_all = n_row * n_col
    full_rows = tile_rows * n_row
    full_cols = tile_cols * n_col
    scales = (
        1.0 / math.sqrt(full_cols * depth),
        1.0 / math.sqrt(full_rows * depth),
        1.0 / math.sqrt(full_rows * full_cols),
    )
    chunk = depth * rank // (n_all * LANES)
    own_a, own_b = a.shape[0], b.shape[0]
    hbm = pl.BlockSpec(memory_space=pl.ANY)
    slots = ITERS * (4 + 2 * HALVES) + 2
    outs = pl.pallas_call(
        functools.partial(kernel, n_row, n_col, scales),
        out_shape=tuple(jax.ShapeDtypeStruct(f.shape, F32) for f in (a, b, c)),
        in_specs=[hbm] * 11,
        out_specs=[hbm] * 3,
        scratch_shapes=[
            pltpu.VMEM(tensor.shape, tensor.dtype),
            pltpu.VMEM((8, tile_cols), jnp.int32),
            pltpu.VMEM((ITERS, n_col, own_a, rank), BF16),
            pltpu.VMEM((n_row, own_b, rank), BF16),
            pltpu.VMEM((ITERS, HALVES, n_row, own_b, half), BF16),
            pltpu.VMEM((ITERS + 1, n_all, chunk, LANES), BF16),
            pltpu.VMEM((ITERS, n_col, own_a, rank), BF16),
            pltpu.VMEM((ITERS, HALVES, n_row, own_b, half), BF16),
            pltpu.VMEM((ITERS, n_all, chunk, LANES), BF16),
            pltpu.VMEM((ITERS, n_col, own_a, rank), BF16),
            pltpu.VMEM((ITERS, HALVES, n_row, own_b, half), BF16),
            pltpu.VMEM((ITERS, n_all, chunk, LANES), BF16),
            pltpu.VMEM((tile_rows, rank), BF16),
            pltpu.VMEM((tile_rows, rank), F32),
            pltpu.VMEM((depth, rank), BF16),
            pltpu.VMEM((depth, rank), F32),
            pltpu.VMEM((tile_rows, rank), F32),
            pltpu.VMEM((tile_cols, rank), F32),
            pltpu.VMEM((depth, rank), F32),
            pltpu.VMEM((3, own_a, rank), F32),
            pltpu.VMEM((3, own_b, rank), F32),
            pltpu.VMEM((3, chunk, LANES), F32),
            pltpu.VMEM((3, n_all, chunk, LANES), F32),
            pltpu.VMEM((tile_rows * depth, rank), BF16),
            pltpu.VMEM((tile_rows * depth, tile_cols), BF16),
            pltpu.VMEM((tile_rows * depth, tile_cols), F32),
            *[pltpu.VMEM(f.shape, F32) for f in (a, b, c)],
            *[pltpu.VMEM(f.shape, F32) for f in (a, b, c, ma, va, mb, vb, mc, vc)],
            pltpu.SemaphoreType.DMA((11,)),
            pltpu.SemaphoreType.DMA((slots,)),
            pltpu.SemaphoreType.DMA((slots,)),
            pltpu.SemaphoreType.DMA((3,)),
        ],
        compiler_params=pltpu.CompilerParams(
            collective_id=0, has_side_effects=True, vmem_limit_bytes=60 * 1024 * 1024
        ),
    )(tensor, loss_kind, a, b, c, ma, va, mb, vb, mc, vc)
    return pl.pallas_call(
        hand_on,
        out_shape=tuple(jax.ShapeDtypeStruct(f.shape, F32) for f in (a, b, c)),
        in_specs=[hbm] * 3,
        out_specs=[hbm] * 3,
        scratch_shapes=[pltpu.SemaphoreType.DMA((3,))],
    )(*outs)


def solution(mesh):
    in_specs = (
        P("row", None, "col"),
        P("row", None, "col"),
        P(("row", "col"), None),
        P(("col", "row"), None),
        P(),
        P(("row", "col"), None),
        P(("row", "col"), None),
        P(("col", "row"), None),
        P(("col", "row"), None),
        P(),
        P(),
    )
    out_specs = (P(("row", "col"), None), P(("col", "row"), None), P())
    return jax.shard_map(shards, mesh=mesh, in_specs=in_specs, out_specs=out_specs, check_vma=False)
```

```python
import functools
import math

import jax
import jax.numpy as jnp
from jax import lax
from jax.experimental import pallas as pl
from jax.experimental.pallas import tpu as pltpu
from jax.sharding import PartitionSpec as P

ITERS = 2
STEP = 10
HALVES = 2
P_ROWS = 16
ROWS = 16
LANES = 128

learn_rate = 0.05
beta_one = 0.8
beta_two = 0.95
adam_eps = 1e-08

F32 = jnp.float32
BF16 = jnp.bfloat16


def adam_step(param, first, second, grad, counter):
    first = beta_one * first + (1.0 - beta_one) * grad
    second = beta_two * second + (1.0 - beta_two) * grad * grad
    corr_one = 1.0 - beta_one**counter
    corr_two = 1.0 - beta_two**counter
    param = param - learn_rate * (first / corr_one) / (jnp.sqrt(second / corr_two) + adam_eps)
    return (param, first, second)


def kernel(
    n_row, n_col, scales,
    tensor, kind, a_hbm, b_hbm, c_hbm, ma_hbm, va_hbm, mb_hbm, vb_hbm, mc_hbm, vc_hbm,
    oa, ob, oc,
    x_s, kind_s, ag_a, ag_b, ag_bh, ag_c, gs_a, gs_b, gs_c, rs_a, rs_b, rs_c,
    a_b, a_f, c_b, c_f, ga, gb, gc, st_a, st_b, st_c, split, p_s, y_s, out_a, out_b, out_c,
    a_in, b_in, c_in, ma_in, va_in, mb_in, vb_in, mc_in, vc_in,
    load_sem, sends, recvs, out_sem,
):
    row = lax.axis_index("row")
    col = lax.axis_index("col")
    n_all = n_row * n_col
    me = row * n_col + col
    tile_rows, depth, tile_cols = x_s.shape
    rank = a_f.shape[1]
    half = rank // HALVES
    own_a = a_in.shape[0]
    own_b = b_in.shape[0]
    chunk = st_c.shape[1]
    groups = rank // LANES

    load_x = pltpu.make_async_copy(tensor, x_s, load_sem.at[0])
    load_k = pltpu.make_async_copy(kind.at[0, pl.ds(0, 8)], kind_s, load_sem.at[1])

    pairs = (
        (a_hbm, a_in), (b_hbm, b_in), (c_hbm, c_in), (ma_hbm, ma_in), (va_hbm, va_in),
        (mb_hbm, mb_in), (vb_hbm, vb_in), (mc_hbm, mc_in), (vc_hbm, vc_in),
    )
    loads = [
        pltpu.make_async_copy(src, dst, load_sem.at[2 + i]) for i, (src, dst) in enumerate(pairs)
    ]

    def device(d):
        return {"row": lax.div(d, n_col), "col": lax.rem(d, n_col)}

    kinds = {
        "a": (n_col, col, lambda d: {"col": d}),
        "b": (n_row, row, lambda d: {"row": d}),
        "c": (n_all, me, device),
    }
    barrier = pltpu.get_barrier_semaphore()

    for what in "ba":
        n, mine, target = kinds[what]

        def greet(k, carry):
            pl.semaphore_signal(
                barrier, inc=1, device_id=target(lax.rem(mine + k, n)),
                device_id_type=pl.DeviceIdType.MESH,
            )
            return carry

        lax.fori_loop(1, n, greet, 0)

    for load in loads:
        load.start()
    load_k.start()
    load_x.start()

    slots = {}

    def copy(src, dst, what, slot, target):
        return pltpu.make_async_remote_copy(
            src_ref=src, dst_ref=dst, send_sem=sends.at[slot], recv_sem=recvs.at[slot],
            device_id=kinds[what][2](target), device_id_type=pl.DeviceIdType.MESH,
        )

    def start(what, key, scatter, src, dst):
        slot = slots[what, key, scatter] = len(slots)
        n, mine, _ = kinds[what]

        def body(k, carry):
            peer = lax.rem(mine + k, n)
            copy(src.at[peer if scatter else mine], dst.at[mine], what, slot, peer).start()
            return carry

        lax.fori_loop(1, n, body, 0)
        started.append((what, key, scatter, src, dst))

    def whole(what, key, scatter, src, dst):
        n, mine, _ = kinds[what]
        part = pl.ds(0, n - 1)
        return copy(
            src.at[part], dst.at[part], what, slots[what, key, scatter], lax.rem(mine + 1, n)
        )

    started = []

    for load in loads[:3]:
        load.wait()
    a = a_in[...]
    b = b_in[...]
    ag_a[0, col] = a.astype(BF16)
    ag_b[row] = b.astype(BF16)

    pl.semaphore_wait(barrier, n_row + n_col - 2)
    start("b", 0, False, ag_b, ag_b)
    start("a", 0, False, ag_a.at[0], ag_a.at[0])

    for load in loads[3:]:
        load.wait()
    for i, ref in enumerate((c_in, mc_in, vc_in)):
        for d in range(n_all):
            g, h = d // groups, d % groups
            split[i, d] = ref[g * chunk : (g + 1) * chunk, h * LANES : (h + 1) * LANES]
    st_a[0], st_a[1], st_a[2] = a, ma_in[...], va_in[...]
    st_b[0], st_b[1], st_b[2] = b, mb_in[...], vb_in[...]
    st_c[0], st_c[1], st_c[2] = split[0, me], split[1, me], split[2, me]
    c_b[...] = c_in[...].astype(BF16)
    load_x.wait()
    load_k.wait()

    def act(m, rows):
        x = x_s[rows].reshape(m.shape).astype(F32)
        huber = jnp.clip(m - x, -1.0, 1.0)
        logit = 0.5 * jnp.tanh(0.5 * m) + jnp.where(x > 0, -0.5, 0.5)
        is_logit = jnp.broadcast_to(kind_s[0:1, :], m.shape) == 1
        return jnp.where(is_logit, logit, huber).astype(BF16)

    def product(p, b):
        return lax.dot_general(p, b, (((1,), (1,)), ((), ())), preferred_element_type=F32)

    spread = learn_rate * ITERS
    for it in range(ITERS):
        last = it == ITERS - 1
        counter = STEP + it + 1

        whole("a", it, False, ag_a.at[it], ag_a.at[it]).wait_recv()
        a_b[...] = ag_a[it].reshape(tile_rows, rank)
        a_f[...] = a_b[...].astype(F32)
        if it > 0:
            whole("c", it, False, ag_c.at[it], ag_c.at[it]).wait_recv()
            for d in range(n_all):
                g, h = d // groups, d % groups
                c_b[g * chunk : (g + 1) * chunk, h * LANES : (h + 1) * LANES] = ag_c[it, d]
        c_f[...] = c_b[...].astype(F32)

        if it == 0:

            def scale_rows(s, carry):
                at = pl.ds(pl.multiple_of(s * P_ROWS, P_ROWS), P_ROWS)
                span = pl.ds(pl.multiple_of(s * P_ROWS * depth, P_ROWS * depth), P_ROWS * depth)
                p = a_b[at, :][:, None, :] * c_b[...][None]
                p_s[span, :] = p.reshape(P_ROWS * depth, rank)
                return carry

            lax.fori_loop(0, tile_rows // P_ROWS, scale_rows, 0)
            whole("b", 0, False, ag_b, ag_b).wait_recv()
            b_f = ag_b[...].reshape(tile_cols, rank)
        else:
            for h in range(HALVES):
                whole("b", (it, h), False, ag_bh.at[it, h], ag_bh.at[it, h]).wait_recv()
            b_f = jnp.concatenate(
                [ag_bh[it, h].reshape(tile_cols, half) for h in range(HALVES)], axis=1
            )

        def forward(s):
            rows = slice(s * ROWS, (s + 1) * ROWS)
            span = slice(s * ROWS * depth, (s + 1) * ROWS * depth)
            if it > 0:
                p = a_b[rows, :][:, None, :] * c_b[...][None]
                p_s[span, :] = p.reshape(ROWS * depth, rank)
            y = act(product(p_s[span, :], b_f), rows)
            y_s[span, :] = y
            return y

        steps = tile_rows // ROWS
        later = forward(0)
        for s in range(steps):
            y = later
            if s < steps - 1:
                later = forward(s + 1)
            rows = slice(s * ROWS, (s + 1) * ROWS)
            z = jnp.dot(y, b_f, preferred_element_type=F32).reshape(ROWS, depth, rank)
            ga[rows, :] = jnp.sum(z * c_f[...][None], axis=1) * scales[0]
            part = jnp.sum(z * a_f[rows, :][:, None, :], axis=0)
            gc[...] = part if s == 0 else gc[...] + part

        for d in range(n_all):
            g, h = d // groups, d % groups
            gs_c[it, d] = (
                gc[g * chunk : (g + 1) * chunk, h * LANES : (h + 1) * LANES] * scales[2]
            ).astype(BF16)
        start("c", it, True, gs_c.at[it], rs_c.at[it])
        rs_c[it, me] = gs_c[it, me]
        gs_a[it] = ga[...].astype(BF16).reshape(n_col, own_a, rank)
        start("a", it, True, gs_a.at[it], rs_a.at[it])

        for h in range(HALVES):
            cut = slice(h * half, (h + 1) * half)
            g = lax.dot_general(
                y_s[...], p_s[:, cut], (((0,), (0,)), ((), ())), preferred_element_type=F32
            ) * scales[1]
            gb[:, cut] = g
            gs_b[it, h] = g.astype(BF16).reshape(n_row, own_b, half)
            start("b", (it, h), True, gs_b.at[it, h], rs_b.at[it, h])

        whole("a", it, True, gs_a.at[it], rs_a.at[it]).wait_recv()
        grad = ga[pl.ds(pl.multiple_of(col * own_a, own_a), own_a), :]
        for k in range(1, n_col):
            grad = grad + rs_a[it, lax.rem(col + k, n_col)].astype(F32)
        st_a[0], st_a[1], st_a[2] = adam_step(st_a[0], st_a[1], st_a[2], grad, counter)
        if last:
            out_a[...] = (a_in[...] - st_a[0]) / spread
            put_a = pltpu.make_async_copy(out_a, oa, out_sem.at[0])
            put_a.start()
        else:
            ag_a[it + 1, col] = st_a[0].astype(BF16)
            start("a", it + 1, False, ag_a.at[it + 1], ag_a.at[it + 1])

        whole("c", it, True, gs_c.at[it], rs_c.at[it]).wait_recv()
        st_c[0], st_c[1], st_c[2] = adam_step(
            st_c[0], st_c[1], st_c[2], jnp.sum(rs_c[it].astype(F32), axis=0), counter
        )
        c = (split[0, me] - st_c[0]) / spread if last else st_c[0]
        ag_c[it + 1, me] = c.astype(BF16)
        start("c", it + 1, False, ag_c.at[it + 1], ag_c.at[it + 1])

        for h in range(HALVES):
            cut = slice(h * half, (h + 1) * half)
            whole("b", (it, h), True, gs_b.at[it, h], rs_b.at[it, h]).wait_recv()
            grad = gb[pl.ds(pl.multiple_of(row * own_b, own_b), own_b), cut]
            for k in range(1, n_row):
                grad = grad + rs_b[it, h, lax.rem(row + k, n_row)].astype(F32)
            f, m, v = adam_step(st_b[0, :, cut], st_b[1, :, cut], st_b[2, :, cut], grad, counter)
            if last:
                out_b[:, cut] = (b_in[:, cut] - f) / spread
            else:
                st_b[0, :, cut], st_b[1, :, cut], st_b[2, :, cut] = f, m, v
                ag_bh[it + 1, h, row] = f.astype(BF16)
                start("b", (it + 1, h), False, ag_bh.at[it + 1, h], ag_bh.at[it + 1, h])
        if last:
            put_b = pltpu.make_async_copy(out_b, ob, out_sem.at[1])
            put_b.start()

    whole("c", ITERS, False, ag_c.at[ITERS], ag_c.at[ITERS]).wait_recv()
    for d in range(n_all):
        g, h = d // groups, d % groups
        out_c[g * chunk : (g + 1) * chunk, h * LANES : (h + 1) * LANES] = ag_c[ITERS, d].astype(F32)
    put_c = pltpu.make_async_copy(out_c, oc, out_sem.at[2])
    put_c.start()
    for args in started:
        whole(*args).wait_send()
    for put in (put_a, put_b, put_c):
        put.wait()


def hand_on(a, b, c, oa, ob, oc):
    oa[...] = a[...]
    ob[...] = b[...]
    oc[...] = c[...]


def shards(tensor, loss_kind, a, b, c, ma, va, mb, vb, mc, vc):
    tile_rows, depth, tile_cols = tensor.shape
    rank = a.shape[1]
    half = rank // HALVES
    n_row = lax.axis_size("row")
    n_col = lax.axis_size("col")
    n_all = n_row * n_col
    full_rows = tile_rows * n_row
    full_cols = tile_cols * n_col
    scales = (
        1.0 / math.sqrt(full_cols * depth),
        1.0 / math.sqrt(full_rows * depth),
        1.0 / math.sqrt(full_rows * full_cols),
    )
    chunk = depth * rank // (n_all * LANES)
    own_a, own_b = a.shape[0], b.shape[0]
    hbm = pl.BlockSpec(memory_space=pl.ANY)
    slots = ITERS * (4 + 2 * HALVES) + 2
    outs = pl.pallas_call(
        functools.partial(kernel, n_row, n_col, scales),
        out_shape=tuple(jax.ShapeDtypeStruct(f.shape, F32) for f in (a, b, c)),
        in_specs=[hbm] * 11,
        out_specs=[hbm] * 3,
        scratch_shapes=[
            pltpu.VMEM(tensor.shape, tensor.dtype),
            pltpu.VMEM((8, tile_cols), jnp.int32),
            pltpu.VMEM((ITERS, n_col, own_a, rank), BF16),
            pltpu.VMEM((n_row, own_b, rank), BF16),
            pltpu.VMEM((ITERS, HALVES, n_row, own_b, half), BF16),
            pltpu.VMEM((ITERS + 1, n_all, chunk, LANES), BF16),
            pltpu.VMEM((ITERS, n_col, own_a, rank), BF16),
            pltpu.VMEM((ITERS, HALVES, n_row, own_b, half), BF16),
            pltpu.VMEM((ITERS, n_all, chunk, LANES), BF16),
            pltpu.VMEM((ITERS, n_col, own_a, rank), BF16),
            pltpu.VMEM((ITERS, HALVES, n_row, own_b, half), BF16),
            pltpu.VMEM((ITERS, n_all, chunk, LANES), BF16),
            pltpu.VMEM((tile_rows, rank), BF16),
            pltpu.VMEM((tile_rows, rank), F32),
            pltpu.VMEM((depth, rank), BF16),
            pltpu.VMEM((depth, rank), F32),
            pltpu.VMEM((tile_rows, rank), F32),
            pltpu.VMEM((tile_cols, rank), F32),
            pltpu.VMEM((depth, rank), F32),
            pltpu.VMEM((3, own_a, rank), F32),
            pltpu.VMEM((3, own_b, rank), F32),
            pltpu.VMEM((3, chunk, LANES), F32),
            pltpu.VMEM((3, n_all, chunk, LANES), F32),
            pltpu.VMEM((tile_rows * depth, rank), BF16),
            pltpu.VMEM((tile_rows * depth, tile_cols), BF16),
            *[pltpu.VMEM(f.shape, F32) for f in (a, b, c)],
            *[pltpu.VMEM(f.shape, F32) for f in (a, b, c, ma, va, mb, vb, mc, vc)],
            pltpu.SemaphoreType.DMA((11,)),
            pltpu.SemaphoreType.DMA((slots,)),
            pltpu.SemaphoreType.DMA((slots,)),
            pltpu.SemaphoreType.DMA((3,)),
        ],
        compiler_params=pltpu.CompilerParams(
            collective_id=0, has_side_effects=True, vmem_limit_bytes=60 * 1024 * 1024
        ),
    )(tensor, loss_kind, a, b, c, ma, va, mb, vb, mc, vc)
    vmem = pl.BlockSpec(memory_space=pltpu.VMEM)
    return pl.pallas_call(
        hand_on,
        out_shape=tuple(jax.ShapeDtypeStruct(f.shape, F32) for f in (a, b, c)),
        in_specs=[vmem] * 3,
        out_specs=[vmem] * 3,
    )(*outs)


def solution(mesh):
    in_specs = (
        P("row", None, "col"),
        P("row", None, "col"),
        P(("row", "col"), None),
        P(("col", "row"), None),
        P(),
        P(("row", "col"), None),
        P(("row", "col"), None),
        P(("col", "row"), None),
        P(("col", "row"), None),
        P(),
        P(),
    )
    out_specs = (P(("row", "col"), None), P(("col", "row"), None), P())
    return jax.shard_map(shards, mesh=mesh, in_specs=in_specs, out_specs=out_specs, check_vma=False)
```

```python
import functools
import math

import jax
import jax.numpy as jnp
from jax import lax
from jax.experimental import pallas as pl
from jax.experimental.pallas import tpu as pltpu
from jax.sharding import PartitionSpec as P

ITERS = 2
STEP = 10
HALVES = 1
P_ROWS = 16
ROWS = 16
LANES = 128

learn_rate = 0.05
beta_one = 0.8
beta_two = 0.95
adam_eps = 1e-08

F32 = jnp.float32
BF16 = jnp.bfloat16


def adam_step(param, first, second, grad, counter):
    first = beta_one * first + (1.0 - beta_one) * grad
    second = beta_two * second + (1.0 - beta_two) * grad * grad
    corr_one = 1.0 - beta_one**counter
    corr_two = 1.0 - beta_two**counter
    param = param - learn_rate * (first / corr_one) / (jnp.sqrt(second / corr_two) + adam_eps)
    return (param, first, second)


def kernel(
    n_row, n_col, scales,
    tensor, kind, a_hbm, b_hbm, c_hbm, ma_hbm, va_hbm, mb_hbm, vb_hbm, mc_hbm, vc_hbm,
    oa, ob, oc,
    x_s, kind_s, ag_a, ag_b, ag_bh, ag_c, gs_a, gs_b, gs_c, rs_a, rs_b, rs_c,
    a_b, a_f, c_b, c_f, ga, gb, gc, st_a, st_b, st_c, split, p_s, y_s, out_a, out_b,
    a_in, b_in, c_in, ma_in, va_in, mb_in, vb_in, mc_in, vc_in,
    load_sem, sends, recvs, out_sem,
):
    row = lax.axis_index("row")
    col = lax.axis_index("col")
    n_all = n_row * n_col
    me = row * n_col + col
    tile_rows, depth, tile_cols = x_s.shape
    rank = a_f.shape[1]
    half = rank // HALVES
    own_a = a_in.shape[0]
    own_b = b_in.shape[0]
    chunk = st_c.shape[1]
    groups = rank // LANES

    load_x = pltpu.make_async_copy(tensor, x_s, load_sem.at[0])
    load_k = pltpu.make_async_copy(kind.at[0, pl.ds(0, 8)], kind_s, load_sem.at[1])

    pairs = (
        (a_hbm, a_in), (b_hbm, b_in), (c_hbm, c_in), (ma_hbm, ma_in), (va_hbm, va_in),
        (mb_hbm, mb_in), (vb_hbm, vb_in), (mc_hbm, mc_in), (vc_hbm, vc_in),
    )
    loads = [
        pltpu.make_async_copy(src, dst, load_sem.at[2 + i]) for i, (src, dst) in enumerate(pairs)
    ]

    def device(d):
        return {"row": lax.div(d, n_col), "col": lax.rem(d, n_col)}

    kinds = {
        "a": (n_col, col, lambda d: {"col": d}),
        "b": (n_row, row, lambda d: {"row": d}),
        "c": (n_all, me, device),
    }
    for load in loads[:2]:
        load.start()
    barrier = pltpu.get_barrier_semaphore()

    for what in "ba":
        n, mine, target = kinds[what]

        def greet(k, carry):
            pl.semaphore_signal(
                barrier, inc=1, device_id=target(lax.rem(mine + k, n)),
                device_id_type=pl.DeviceIdType.MESH,
            )
            return carry

        lax.fori_loop(1, n, greet, 0)

    for load in loads[2:]:
        load.start()
    load_k.start()
    load_x.start()

    slots = {}

    def copy(src, dst, what, slot, target):
        return pltpu.make_async_remote_copy(
            src_ref=src, dst_ref=dst, send_sem=sends.at[slot], recv_sem=recvs.at[slot],
            device_id=kinds[what][2](target), device_id_type=pl.DeviceIdType.MESH,
        )

    def start(what, key, scatter, src, dst):
        slot = slots[what, key, scatter] = len(slots)
        n, mine, _ = kinds[what]

        def body(k, carry):
            peer = lax.rem(mine + k, n)
            copy(src.at[peer if scatter else mine], dst.at[mine], what, slot, peer).start()
            return carry

        lax.fori_loop(1, n, body, 0)
        started.append((what, key, scatter, src, dst))

    def whole(what, key, scatter, src, dst):
        n, mine, _ = kinds[what]
        part = pl.ds(0, n - 1)
        return copy(
            src.at[part], dst.at[part], what, slots[what, key, scatter], lax.rem(mine + 1, n)
        )

    started = []

    for load in loads[:2]:
        load.wait()
    a = a_in[...]
    b = b_in[...]
    ag_a[0, col] = a.astype(BF16)
    ag_b[row] = b.astype(BF16)

    pl.semaphore_wait(barrier, n_row + n_col - 2)
    start("b", 0, False, ag_b, ag_b)
    start("a", 0, False, ag_a.at[0], ag_a.at[0])

    for load in loads[2:]:
        load.wait()
    for i, ref in enumerate((c_in, mc_in, vc_in)):
        for d in range(n_all):
            g, h = d // groups, d % groups
            split[i, d] = ref[g * chunk : (g + 1) * chunk, h * LANES : (h + 1) * LANES]
    st_a[0], st_a[1], st_a[2] = a, ma_in[...], va_in[...]
    st_b[0], st_b[1], st_b[2] = b, mb_in[...], vb_in[...]
    st_c[0], st_c[1], st_c[2] = split[0, me], split[1, me], split[2, me]
    c_b[...] = c_in[...].astype(BF16)
    load_x.wait()
    load_k.wait()

    def act(m, rows):
        x = x_s[rows].reshape(m.shape).astype(F32)
        huber = jnp.clip(m - x, -1.0, 1.0)
        logit = 0.5 * jnp.tanh(0.5 * m) + jnp.where(x > 0, -0.5, 0.5)
        is_logit = jnp.broadcast_to(kind_s[0:1, :], m.shape) == 1
        return jnp.where(is_logit, logit, huber).astype(BF16)

    def product(p, b):
        return lax.dot_general(p, b, (((1,), (1,)), ((), ())), preferred_element_type=F32)

    spread = learn_rate * ITERS
    for it in range(ITERS):
        last = it == ITERS - 1
        counter = STEP + it + 1

        whole("a", it, False, ag_a.at[it], ag_a.at[it]).wait_recv()
        a_b[...] = ag_a[it].reshape(tile_rows, rank)
        a_f[...] = a_b[...].astype(F32)
        if it > 0:
            whole("c", it, False, ag_c.at[it], ag_c.at[it]).wait_recv()
            for d in range(n_all):
                g, h = d // groups, d % groups
                c_b[g * chunk : (g + 1) * chunk, h * LANES : (h + 1) * LANES] = ag_c[it, d]
        c_f[...] = c_b[...].astype(F32)

        def scale_rows(s, carry):
            at = pl.ds(pl.multiple_of(s * P_ROWS, P_ROWS), P_ROWS)
            span = pl.ds(pl.multiple_of(s * P_ROWS * depth, P_ROWS * depth), P_ROWS * depth)
            p = a_b[at, :][:, None, :] * c_b[...][None]
            p_s[span, :] = p.reshape(P_ROWS * depth, rank)
            return carry

        lax.fori_loop(0, tile_rows // P_ROWS, scale_rows, 0)

        if it == 0:
            whole("b", 0, False, ag_b, ag_b).wait_recv()
            b_f = ag_b[...].reshape(tile_cols, rank)
        else:
            for h in range(HALVES):
                whole("b", (it, h), False, ag_bh.at[it, h], ag_bh.at[it, h]).wait_recv()
            b_f = jnp.concatenate(
                [ag_bh[it, h].reshape(tile_cols, half) for h in range(HALVES)], axis=1
            )

        def forward(s):
            rows = slice(s * ROWS, (s + 1) * ROWS)
            span = slice(s * ROWS * depth, (s + 1) * ROWS * depth)
            y = act(product(p_s[span, :], b_f), rows)
            y_s[span, :] = y
            return y

        steps = tile_rows // ROWS
        later = forward(0)
        for s in range(steps):
            y = later
            if s < steps - 1:
                later = forward(s + 1)
            rows = slice(s * ROWS, (s + 1) * ROWS)
            z = jnp.dot(y, b_f, preferred_element_type=F32).reshape(ROWS, depth, rank)
            ga[rows, :] = jnp.sum(z * c_f[...][None], axis=1) * scales[0]
            part = jnp.sum(z * a_f[rows, :][:, None, :], axis=0)
            gc[...] = part if s == 0 else gc[...] + part

        for d in range(n_all):
            g, h = d // groups, d % groups
            gs_c[it, d] = (
                gc[g * chunk : (g + 1) * chunk, h * LANES : (h + 1) * LANES] * scales[2]
            ).astype(BF16)
        start("c", it, True, gs_c.at[it], rs_c.at[it])
        rs_c[it, me] = gs_c[it, me]

        for h in range(HALVES):
            cut = slice(h * half, (h + 1) * half)
            g = lax.dot_general(
                y_s[...], p_s[:, cut], (((0,), (0,)), ((), ())), preferred_element_type=F32
            ) * scales[1]
            gb[:, cut] = g
            gs_b[it, h] = g.astype(BF16).reshape(n_row, own_b, half)
            start("b", (it, h), True, gs_b.at[it, h], rs_b.at[it, h])

        gs_a[it] = ga[...].astype(BF16).reshape(n_col, own_a, rank)
        start("a", it, True, gs_a.at[it], rs_a.at[it])

        whole("c", it, True, gs_c.at[it], rs_c.at[it]).wait_recv()
        st_c[0], st_c[1], st_c[2] = adam_step(
            st_c[0], st_c[1], st_c[2], jnp.sum(rs_c[it].astype(F32), axis=0), counter
        )
        c = (split[0, me] - st_c[0]) / spread if last else st_c[0]
        ag_c[it + 1, me] = c.astype(BF16)
        land = oc if last else ag_c.at[it + 1]
        start("c", it + 1, False, ag_c.at[it + 1], land)
        if last:
            put_c = pltpu.make_async_copy(ag_c.at[it + 1, me], oc.at[me], out_sem.at[2])
            put_c.start()

        whole("a", it, True, gs_a.at[it], rs_a.at[it]).wait_recv()
        grad = ga[pl.ds(pl.multiple_of(col * own_a, own_a), own_a), :]
        for k in range(1, n_col):
            grad = grad + rs_a[it, lax.rem(col + k, n_col)].astype(F32)
        st_a[0], st_a[1], st_a[2] = adam_step(st_a[0], st_a[1], st_a[2], grad, counter)
        if last:
            out_a[...] = (a_in[...] - st_a[0]) / spread
            put_a = pltpu.make_async_copy(out_a, oa, out_sem.at[0])
            put_a.start()
        else:
            ag_a[it + 1, col] = st_a[0].astype(BF16)
            start("a", it + 1, False, ag_a.at[it + 1], ag_a.at[it + 1])

        for h in range(HALVES):
            cut = slice(h * half, (h + 1) * half)
            whole("b", (it, h), True, gs_b.at[it, h], rs_b.at[it, h]).wait_recv()
            grad = gb[pl.ds(pl.multiple_of(row * own_b, own_b), own_b), cut]
            for k in range(1, n_row):
                grad = grad + rs_b[it, h, lax.rem(row + k, n_row)].astype(F32)
            f, m, v = adam_step(st_b[0, :, cut], st_b[1, :, cut], st_b[2, :, cut], grad, counter)
            if last:
                out_b[:, cut] = (b_in[:, cut] - f) / spread
            else:
                st_b[0, :, cut], st_b[1, :, cut], st_b[2, :, cut] = f, m, v
                ag_bh[it + 1, h, row] = f.astype(BF16)
                start("b", (it + 1, h), False, ag_bh.at[it + 1, h], ag_bh.at[it + 1, h])
        if last:
            put_b = pltpu.make_async_copy(out_b, ob, out_sem.at[1])
            put_b.start()

    whole("c", ITERS, False, ag_c.at[ITERS], oc).wait_recv()
    for args in started:
        whole(*args).wait_send()
    for put in (put_a, put_b, put_c):
        put.wait()


def hand_on(a, b, c, oa, ob, oc):
    oa[...] = a[...]
    ob[...] = b[...]
    chunk = c.shape[1]
    groups = oc.shape[1] // LANES
    for d in range(c.shape[0]):
        g, h = d // groups, d % groups
        oc[g * chunk : (g + 1) * chunk, h * LANES : (h + 1) * LANES] = c[d].astype(F32)


def shards(tensor, loss_kind, a, b, c, ma, va, mb, vb, mc, vc):
    tile_rows, depth, tile_cols = tensor.shape
    rank = a.shape[1]
    half = rank // HALVES
    n_row = lax.axis_size("row")
    n_col = lax.axis_size("col")
    n_all = n_row * n_col
    full_rows = tile_rows * n_row
    full_cols = tile_cols * n_col
    scales = (
        1.0 / math.sqrt(full_cols * depth),
        1.0 / math.sqrt(full_rows * depth),
        1.0 / math.sqrt(full_rows * full_cols),
    )
    chunk = depth * rank // (n_all * LANES)
    own_a, own_b = a.shape[0], b.shape[0]
    hbm = pl.BlockSpec(memory_space=pl.ANY)
    slots = ITERS * (4 + 2 * HALVES) + 2
    outs = pl.pallas_call(
        functools.partial(kernel, n_row, n_col, scales),
        out_shape=(
            jax.ShapeDtypeStruct(a.shape, F32),
            jax.ShapeDtypeStruct(b.shape, F32),
            jax.ShapeDtypeStruct((n_all, chunk, LANES), BF16),
        ),
        in_specs=[hbm] * 11,
        out_specs=[hbm] * 3,
        scratch_shapes=[
            pltpu.VMEM(tensor.shape, tensor.dtype),
            pltpu.VMEM((8, tile_cols), jnp.int32),
            pltpu.VMEM((ITERS, n_col, own_a, rank), BF16),
            pltpu.VMEM((n_row, own_b, rank), BF16),
            pltpu.VMEM((ITERS, HALVES, n_row, own_b, half), BF16),
            pltpu.VMEM((ITERS + 1, n_all, chunk, LANES), BF16),
            pltpu.VMEM((ITERS, n_col, own_a, rank), BF16),
            pltpu.VMEM((ITERS, HALVES, n_row, own_b, half), BF16),
            pltpu.VMEM((ITERS, n_all, chunk, LANES), BF16),
            pltpu.VMEM((ITERS, n_col, own_a, rank), BF16),
            pltpu.VMEM((ITERS, HALVES, n_row, own_b, half), BF16),
            pltpu.VMEM((ITERS, n_all, chunk, LANES), BF16),
            pltpu.VMEM((tile_rows, rank), BF16),
            pltpu.VMEM((tile_rows, rank), F32),
            pltpu.VMEM((depth, rank), BF16),
            pltpu.VMEM((depth, rank), F32),
            pltpu.VMEM((tile_rows, rank), F32),
            pltpu.VMEM((tile_cols, rank), F32),
            pltpu.VMEM((depth, rank), F32),
            pltpu.VMEM((3, own_a, rank), F32),
            pltpu.VMEM((3, own_b, rank), F32),
            pltpu.VMEM((3, chunk, LANES), F32),
            pltpu.VMEM((3, n_all, chunk, LANES), F32),
            pltpu.VMEM((tile_rows * depth, rank), BF16),
            pltpu.VMEM((tile_rows * depth, tile_cols), BF16),
            *[pltpu.VMEM(f.shape, F32) for f in (a, b)],
            *[pltpu.VMEM(f.shape, F32) for f in (a, b, c, ma, va, mb, vb, mc, vc)],
            pltpu.SemaphoreType.DMA((11,)),
            pltpu.SemaphoreType.DMA((slots,)),
            pltpu.SemaphoreType.DMA((slots,)),
            pltpu.SemaphoreType.DMA((3,)),
        ],
        compiler_params=pltpu.CompilerParams(
            collective_id=0, has_side_effects=True, vmem_limit_bytes=60 * 1024 * 1024
        ),
    )(tensor, loss_kind, a, b, c, ma, va, mb, vb, mc, vc)
    vmem = pl.BlockSpec(memory_space=pltpu.VMEM)
    return pl.pallas_call(
        hand_on,
        out_shape=tuple(jax.ShapeDtypeStruct(f.shape, F32) for f in (a, b, c)),
        in_specs=[vmem] * 3,
        out_specs=[vmem] * 3,
    )(*outs)


def solution(mesh):
    in_specs = (
        P("row", None, "col"),
        P("row", None, "col"),
        P(("row", "col"), None),
        P(("col", "row"), None),
        P(),
        P(("row", "col"), None),
        P(("row", "col"), None),
        P(("col", "row"), None),
        P(("col", "row"), None),
        P(),
        P(),
    )
    out_specs = (P(("row", "col"), None), P(("col", "row"), None), P())
    return jax.shard_map(shards, mesh=mesh, in_specs=in_specs, out_specs=out_specs, check_vma=False)
```

```python
import functools
import math

import jax
import jax.numpy as jnp
from jax import lax
from jax.experimental import pallas as pl
from jax.experimental.pallas import tpu as pltpu
from jax.sharding import PartitionSpec as P

ITERS = 2
STEP = 10
HALVES = 1
P_ROWS = 16
DEEP = 8
TURN = 4
PAD = 8
LANES = 128

learn_rate = 0.05
beta_one = 0.8
beta_two = 0.95
adam_eps = 1e-08

F32 = jnp.float32
BF16 = jnp.bfloat16


def adam_step(param, first, second, grad, counter):
    first = beta_one * first + (1.0 - beta_one) * grad
    second = beta_two * second + (1.0 - beta_two) * grad * grad
    corr_one = 1.0 - beta_one**counter
    corr_two = 1.0 - beta_two**counter
    param = param - learn_rate * (first / corr_one) / (jnp.sqrt(second / corr_two) + adam_eps)
    return (param, first, second)


def kernel(
    n_row, n_col, scales,
    tensor, kind, a_hbm, b_hbm, c_hbm, ma_hbm, va_hbm, mb_hbm, vb_hbm, mc_hbm, vc_hbm,
    oa, ob, oc,
    x_s, x_f, x_t, kind_s, ag_a, ag_b, ag_bh, ag_c, gs_a, gs_b, gs_c, rs_a, rs_b, rs_c,
    a_b, a_f, c_b, c_f, ga, gb, st_a, st_b, st_c, split, p_s, y_s, out_a, out_b,
    a_in, b_in, c_in, ma_in, va_in, mb_in, vb_in, mc_in, vc_in,
    load_sem, sends, recvs, out_sem,
):
    row = lax.axis_index("row")
    col = lax.axis_index("col")
    n_all = n_row * n_col
    me = row * n_col + col
    tile_rows, depth, tile_cols = x_s.shape
    rank = a_f.shape[1]
    half = rank // HALVES
    own_a = a_in.shape[0]
    own_b = b_in.shape[0]
    chunk = st_c.shape[1]
    groups = rank // LANES

    load_x = pltpu.make_async_copy(tensor, x_s, load_sem.at[0])
    load_k = pltpu.make_async_copy(kind.at[0, pl.ds(0, 8)], kind_s, load_sem.at[1])

    pairs = (
        (a_hbm, a_in), (b_hbm, b_in), (c_hbm, c_in), (ma_hbm, ma_in), (va_hbm, va_in),
        (mb_hbm, mb_in), (vb_hbm, vb_in), (mc_hbm, mc_in), (vc_hbm, vc_in),
    )
    loads = [
        pltpu.make_async_copy(src, dst, load_sem.at[2 + i]) for i, (src, dst) in enumerate(pairs)
    ]

    def device(d):
        return {"row": lax.div(d, n_col), "col": lax.rem(d, n_col)}

    kinds = {
        "a": (n_col, col, lambda d: {"col": d}),
        "b": (n_row, row, lambda d: {"row": d}),
        "c": (n_all, me, device),
    }
    for load in loads[:2]:
        load.start()
    barrier = pltpu.get_barrier_semaphore()

    for what in "ba":
        n, mine, target = kinds[what]

        def greet(k, carry):
            pl.semaphore_signal(
                barrier, inc=1, device_id=target(lax.rem(mine + k, n)),
                device_id_type=pl.DeviceIdType.MESH,
            )
            return carry

        lax.fori_loop(1, n, greet, 0)

    for load in loads[2:]:
        load.start()
    load_k.start()
    load_x.start()

    slots = {}

    def copy(src, dst, what, slot, target):
        return pltpu.make_async_remote_copy(
            src_ref=src, dst_ref=dst, send_sem=sends.at[slot], recv_sem=recvs.at[slot],
            device_id=kinds[what][2](target), device_id_type=pl.DeviceIdType.MESH,
        )

    def start(what, key, scatter, src, dst):
        slot = slots[what, key, scatter] = len(slots)
        n, mine, _ = kinds[what]

        def body(k, carry):
            peer = lax.rem(mine + k, n)
            copy(src.at[peer if scatter else mine], dst.at[mine], what, slot, peer).start()
            return carry

        lax.fori_loop(1, n, body, 0)
        started.append((what, key, scatter, src, dst))

    def whole(what, key, scatter, src, dst):
        n, mine, _ = kinds[what]
        part = pl.ds(0, n - 1)
        return copy(
            src.at[part], dst.at[part], what, slots[what, key, scatter], lax.rem(mine + 1, n)
        )

    started = []

    for load in loads[:2]:
        load.wait()
    a = a_in[...]
    b = b_in[...]
    ag_a[0, col] = a.astype(BF16)
    ag_b[row] = b.astype(BF16)

    pl.semaphore_wait(barrier, n_row + n_col - 2)
    start("b", 0, False, ag_b, ag_b)
    start("a", 0, False, ag_a.at[0], ag_a.at[0])

    for load in loads[2:]:
        load.wait()
    for i, ref in enumerate((c_in, mc_in, vc_in)):
        for d in range(n_all):
            g, h = d // groups, d % groups
            split[i, d] = ref[g * chunk : (g + 1) * chunk, h * LANES : (h + 1) * LANES]
    st_a[0], st_a[1], st_a[2] = a, ma_in[...], va_in[...]
    st_b[0], st_b[1], st_b[2] = b, mb_in[...], vb_in[...]
    st_c[0], st_c[1], st_c[2] = split[0, me], split[1, me], split[2, me]
    c_b[...] = c_in[...].astype(BF16)
    load_x.wait()
    load_k.wait()

    pitch = x_f.shape[0] // tile_rows

    def widen(s, carry):
        for u in range(P_ROWS):
            i = s * P_ROWS + u
            x_f[pl.ds(pl.multiple_of(i * pitch, 8), depth), :] = x_s[i].astype(F32)
        return carry

    lax.fori_loop(0, tile_rows // P_ROWS, widen, 0)

    def turn(s, carry):
        for u in range(TURN):
            k = s * TURN + u
            x_t[k] = x_f[pl.ds(k, tile_rows, stride=pitch), :].astype(BF16)
        return carry

    lax.fori_loop(0, depth // TURN, turn, 0)

    steps = depth // DEEP
    per_step = n_all // steps
    mine_step = lax.div(me, per_step)

    def step_at(s):
        if steps & (steps - 1):
            return lax.rem(mine_step + 1 + s, steps)
        at = mine_step
        for bit in (1 << i for i in range(steps.bit_length() - 1)):
            if (steps - 1 - s) & bit:
                at = at + bit * (1 - 2 * lax.rem(lax.div(mine_step, bit), 2))
        return at

    def act(m, x):
        x = x.astype(F32)
        huber = jnp.clip(m - x, -1.0, 1.0)
        logit = 0.5 * jnp.tanh(0.5 * m) + jnp.where(x > 0, -0.5, 0.5)
        is_logit = jnp.broadcast_to(kind_s[0:1, :], m.shape) == 1
        return jnp.where(is_logit, logit, huber).astype(BF16)

    def product(p, b):
        return lax.dot_general(p, b, (((1,), (1,)), ((), ())), preferred_element_type=F32)

    spread = learn_rate * ITERS
    for it in range(ITERS):
        last = it == ITERS - 1
        counter = STEP + it + 1

        whole("a", it, False, ag_a.at[it], ag_a.at[it]).wait_recv()
        a_b[...] = ag_a[it].reshape(tile_rows, rank)
        a_f[...] = a_b[...].astype(F32)
        if it > 0:
            whole("c", it, False, ag_c.at[it], ag_c.at[it]).wait_recv()
            for d in range(n_all):
                g, h = d // groups, d % groups
                c_b[g * chunk : (g + 1) * chunk, h * LANES : (h + 1) * LANES] = ag_c[it, d]
        c_f[...] = c_b[...].astype(F32)

        def scale_rows(s, carry):
            at = pl.ds(pl.multiple_of(s * P_ROWS, P_ROWS), P_ROWS)
            wide = P_ROWS * tile_rows
            p = c_b[at, :][:, None, :] * a_b[...][None]
            p_s[pl.ds(pl.multiple_of(s * wide, wide), wide), :] = p.reshape(wide, rank)
            return carry

        lax.fori_loop(0, depth // P_ROWS, scale_rows, 0)

        if it == 0:
            whole("b", 0, False, ag_b, ag_b).wait_recv()
            b_f = ag_b[...].reshape(tile_cols, rank)
        else:
            for h in range(HALVES):
                whole("b", (it, h), False, ag_bh.at[it, h], ag_bh.at[it, h]).wait_recv()
            b_f = jnp.concatenate(
                [ag_bh[it, h].reshape(tile_cols, half) for h in range(HALVES)], axis=1
            )

        wide = DEEP * tile_rows

        def forward(g):
            span = pl.ds(pl.multiple_of(g * wide, wide), wide)
            x = x_t[pl.ds(pl.multiple_of(g * DEEP, DEEP), DEEP)].reshape(wide, tile_cols)
            y = act(product(p_s[span, :], b_f), x)
            y_s[span, :] = y
            return y

        slot = slots["c", it, True] = len(slots)
        started.append(("c", it, True, gs_c.at[it], rs_c.at[it]))
        later = forward(step_at(0))
        for s in range(steps):
            g = step_at(s)
            y = later
            if s < steps - 1:
                later = forward(step_at(s + 1))
            z = jnp.dot(y, b_f, preferred_element_type=F32).reshape(DEEP, tile_rows, rank)
            c_rows = c_f[pl.ds(pl.multiple_of(g * DEEP, DEEP), DEEP), :]
            part = jnp.sum(z * c_rows[:, None, :], axis=0)
            ga[...] = part if s == 0 else ga[...] + part
            part = (jnp.sum(z * a_f[...][None], axis=1) * scales[2]).astype(BF16)
            for q in range(per_step):
                u, h = q // groups, q % groups
                gs_c[it, g * per_step + q] = part[
                    u * chunk : (u + 1) * chunk, h * LANES : (h + 1) * LANES
                ]
            for t in range(steps // 2) if s == steps // 2 else range(steps // 2, steps) if s == steps - 1 else ():
                far = step_at(t)
                for q in range(per_step):
                    if t == steps - 1 and q == 0:
                        continue
                    peer = far * per_step + lax.rem(me - mine_step * per_step + q, per_step)
                    copy(gs_c.at[it, peer], rs_c.at[it, me], "c", slot, peer).start()

        rs_c[it, me] = gs_c[it, me]

        for h in range(HALVES):
            cut = slice(h * half, (h + 1) * half)
            g = lax.dot_general(
                y_s[...], p_s[:, cut], (((0,), (0,)), ((), ())), preferred_element_type=F32
            ) * scales[1]
            gb[:, cut] = g
            gs_b[it, h] = g.astype(BF16).reshape(n_row, own_b, half)
            start("b", (it, h), True, gs_b.at[it, h], rs_b.at[it, h])

        ga[...] = ga[...] * scales[0]
        gs_a[it] = ga[...].astype(BF16).reshape(n_col, own_a, rank)
        start("a", it, True, gs_a.at[it], rs_a.at[it])

        whole("c", it, True, gs_c.at[it], rs_c.at[it]).wait_recv()
        st_c[0], st_c[1], st_c[2] = adam_step(
            st_c[0], st_c[1], st_c[2], jnp.sum(rs_c[it].astype(F32), axis=0), counter
        )
        c = (split[0, me] - st_c[0]) / spread if last else st_c[0]
        ag_c[it + 1, me] = c.astype(BF16)
        land = oc if last else ag_c.at[it + 1]
        start("c", it + 1, False, ag_c.at[it + 1], land)
        if last:
            put_c = pltpu.make_async_copy(ag_c.at[it + 1, me], oc.at[me], out_sem.at[2])
            put_c.start()

        whole("a", it, True, gs_a.at[it], rs_a.at[it]).wait_recv()
        grad = ga[pl.ds(pl.multiple_of(col * own_a, own_a), own_a), :]
        for k in range(1, n_col):
            grad = grad + rs_a[it, lax.rem(col + k, n_col)].astype(F32)
        st_a[0], st_a[1], st_a[2] = adam_step(st_a[0], st_a[1], st_a[2], grad, counter)
        if last:
            out_a[...] = (a_in[...] - st_a[0]) / spread
            put_a = pltpu.make_async_copy(out_a, oa, out_sem.at[0])
            put_a.start()
        else:
            ag_a[it + 1, col] = st_a[0].astype(BF16)
            start("a", it + 1, False, ag_a.at[it + 1], ag_a.at[it + 1])

        for h in range(HALVES):
            cut = slice(h * half, (h + 1) * half)
            whole("b", (it, h), True, gs_b.at[it, h], rs_b.at[it, h]).wait_recv()
            grad = gb[pl.ds(pl.multiple_of(row * own_b, own_b), own_b), cut]
            for k in range(1, n_row):
                grad = grad + rs_b[it, h, lax.rem(row + k, n_row)].astype(F32)
            f, m, v = adam_step(st_b[0, :, cut], st_b[1, :, cut], st_b[2, :, cut], grad, counter)
            if last:
                out_b[:, cut] = (b_in[:, cut] - f) / spread
            else:
                st_b[0, :, cut], st_b[1, :, cut], st_b[2, :, cut] = f, m, v
                ag_bh[it + 1, h, row] = f.astype(BF16)
                start("b", (it + 1, h), False, ag_bh.at[it + 1, h], ag_bh.at[it + 1, h])
        if last:
            put_b = pltpu.make_async_copy(out_b, ob, out_sem.at[1])
            put_b.start()

    whole("c", ITERS, False, ag_c.at[ITERS], oc).wait_recv()
    for args in started:
        whole(*args).wait_send()
    for put in (put_a, put_b, put_c):
        put.wait()


def hand_on(a, b, c, oa, ob, oc):
    oa[...] = a[...]
    ob[...] = b[...]
    chunk = c.shape[1]
    groups = oc.shape[1] // LANES
    for d in range(c.shape[0]):
        g, h = d // groups, d % groups
        oc[g * chunk : (g + 1) * chunk, h * LANES : (h + 1) * LANES] = c[d].astype(F32)


def shards(tensor, loss_kind, a, b, c, ma, va, mb, vb, mc, vc):
    tile_rows, depth, tile_cols = tensor.shape
    rank = a.shape[1]
    half = rank // HALVES
    n_row = lax.axis_size("row")
    n_col = lax.axis_size("col")
    n_all = n_row * n_col
    full_rows = tile_rows * n_row
    full_cols = tile_cols * n_col
    scales = (
        1.0 / math.sqrt(full_cols * depth),
        1.0 / math.sqrt(full_rows * depth),
        1.0 / math.sqrt(full_rows * full_cols),
    )
    chunk = depth * rank // (n_all * LANES)
    own_a, own_b = a.shape[0], b.shape[0]
    hbm = pl.BlockSpec(memory_space=pl.ANY)
    slots = ITERS * (4 + 2 * HALVES) + 2
    outs = pl.pallas_call(
        functools.partial(kernel, n_row, n_col, scales),
        out_shape=(
            jax.ShapeDtypeStruct(a.shape, F32),
            jax.ShapeDtypeStruct(b.shape, F32),
            jax.ShapeDtypeStruct((n_all, chunk, LANES), BF16),
        ),
        in_specs=[hbm] * 11,
        out_specs=[hbm] * 3,
        scratch_shapes=[
            pltpu.VMEM(tensor.shape, tensor.dtype),
            pltpu.VMEM((tile_rows * (depth + PAD) + depth, tile_cols), F32),
            pltpu.VMEM((depth, tile_rows, tile_cols), tensor.dtype),
            pltpu.VMEM((8, tile_cols), jnp.int32),
            pltpu.VMEM((ITERS, n_col, own_a, rank), BF16),
            pltpu.VMEM((n_row, own_b, rank), BF16),
            pltpu.VMEM((ITERS, HALVES, n_row, own_b, half), BF16),
            pltpu.VMEM((ITERS + 1, n_all, chunk, LANES), BF16),
            pltpu.VMEM((ITERS, n_col, own_a, rank), BF16),
            pltpu.VMEM((ITERS, HALVES, n_row, own_b, half), BF16),
            pltpu.VMEM((ITERS, n_all, chunk, LANES), BF16),
            pltpu.VMEM((ITERS, n_col, own_a, rank), BF16),
            pltpu.VMEM((ITERS, HALVES, n_row, own_b, half), BF16),
            pltpu.VMEM((ITERS, n_all, chunk, LANES), BF16),
            pltpu.VMEM((tile_rows, rank), BF16),
            pltpu.VMEM((tile_rows, rank), F32),
            pltpu.VMEM((depth, rank), BF16),
            pltpu.VMEM((depth, rank), F32),
            pltpu.VMEM((tile_rows, rank), F32),
            pltpu.VMEM((tile_cols, rank), F32),
            pltpu.VMEM((3, own_a, rank), F32),
            pltpu.VMEM((3, own_b, rank), F32),
            pltpu.VMEM((3, chunk, LANES), F32),
            pltpu.VMEM((3, n_all, chunk, LANES), F32),
            pltpu.VMEM((tile_rows * depth, rank), BF16),
            pltpu.VMEM((tile_rows * depth, tile_cols), BF16),
            *[pltpu.VMEM(f.shape, F32) for f in (a, b)],
            *[pltpu.VMEM(f.shape, F32) for f in (a, b, c, ma, va, mb, vb, mc, vc)],
            pltpu.SemaphoreType.DMA((11,)),
            pltpu.SemaphoreType.DMA((slots,)),
            pltpu.SemaphoreType.DMA((slots,)),
            pltpu.SemaphoreType.DMA((3,)),
        ],
        compiler_params=pltpu.CompilerParams(
            collective_id=0, has_side_effects=True, vmem_limit_bytes=60 * 1024 * 1024
        ),
    )(tensor, loss_kind, a, b, c, ma, va, mb, vb, mc, vc)
    vmem = pl.BlockSpec(memory_space=pltpu.VMEM)
    return pl.pallas_call(
        hand_on,
        out_shape=tuple(jax.ShapeDtypeStruct(f.shape, F32) for f in (a, b, c)),
        in_specs=[vmem] * 3,
        out_specs=[vmem] * 3,
    )(*outs)


def solution(mesh):
    in_specs = (
        P("row", None, "col"),
        P("row", None, "col"),
        P(("row", "col"), None),
        P(("col", "row"), None),
        P(),
        P(("row", "col"), None),
        P(("row", "col"), None),
        P(("col", "row"), None),
        P(("col", "row"), None),
        P(),
        P(),
    )
    out_specs = (P(("row", "col"), None), P(("col", "row"), None), P())
    return jax.shard_map(shards, mesh=mesh, in_specs=in_specs, out_specs=out_specs, check_vma=False)
```

```python
import functools
import math

import jax
import jax.numpy as jnp
from jax import lax
from jax.experimental import pallas as pl
from jax.experimental.pallas import tpu as pltpu
from jax.sharding import PartitionSpec as P

ITERS = 2
STEP = 10
HALVES = 1
P_ROWS = 16
DEEP = 8
TURN = 4
PAD = 8
LANES = 128

learn_rate = 0.05
beta_one = 0.8
beta_two = 0.95
adam_eps = 1e-08

F32 = jnp.float32
BF16 = jnp.bfloat16


def adam_step(param, first, second, grad, counter):
    first = beta_one * first + (1.0 - beta_one) * grad
    second = beta_two * second + (1.0 - beta_two) * grad * grad
    corr_one = 1.0 - beta_one**counter
    corr_two = 1.0 - beta_two**counter
    param = param - learn_rate * (first / corr_one) / (jnp.sqrt(second / corr_two) + adam_eps)
    return (param, first, second)


def kernel(
    n_row, n_col, scales,
    tensor, kind, a_hbm, b_hbm, c_hbm, ma_hbm, va_hbm, mb_hbm, vb_hbm, mc_hbm, vc_hbm,
    oa, ob, oc,
    x_s, x_f, x_t, kind_s, ag_a, ag_b, ag_bh, ag_c, gs_a, gs_b, gs_c, rs_a, rs_b, rs_c,
    a_b, a_f, c_b, c_f, ga, gb, st_a, st_b, st_c, split, p_s, y_s, out_a, out_b,
    a_in, b_in, c_in, ma_in, va_in, mb_in, vb_in, mc_in, vc_in,
    load_sem, sends, recvs, out_sem,
):
    row = lax.axis_index("row")
    col = lax.axis_index("col")
    n_all = n_row * n_col
    me = row * n_col + col
    tile_rows, depth, tile_cols = x_s.shape
    rank = a_f.shape[1]
    half = rank // HALVES
    own_a = a_in.shape[0]
    own_b = b_in.shape[0]
    chunk = st_c.shape[1]
    groups = rank // LANES

    load_x = pltpu.make_async_copy(tensor, x_s, load_sem.at[0])
    load_k = pltpu.make_async_copy(kind.at[0, pl.ds(0, 8)], kind_s, load_sem.at[1])

    pairs = (
        (a_hbm, a_in), (b_hbm, b_in), (c_hbm, c_in), (ma_hbm, ma_in), (va_hbm, va_in),
        (mb_hbm, mb_in), (vb_hbm, vb_in), (mc_hbm, mc_in), (vc_hbm, vc_in),
    )
    loads = [
        pltpu.make_async_copy(src, dst, load_sem.at[2 + i]) for i, (src, dst) in enumerate(pairs)
    ]

    def device(d):
        return {"row": lax.div(d, n_col), "col": lax.rem(d, n_col)}

    kinds = {
        "a": (n_col, col, lambda d: {"col": d}),
        "b": (n_row, row, lambda d: {"row": d}),
        "c": (n_all, me, device),
    }
    for load in loads[:2]:
        load.start()
    barrier = pltpu.get_barrier_semaphore()

    for what in "ba":
        n, mine, target = kinds[what]

        def greet(k, carry):
            pl.semaphore_signal(
                barrier, inc=1, device_id=target(lax.rem(mine + k, n)),
                device_id_type=pl.DeviceIdType.MESH,
            )
            return carry

        lax.fori_loop(1, n, greet, 0)

    for load in loads[2:]:
        load.start()
    load_k.start()
    load_x.start()

    slots = {}

    def copy(src, dst, what, slot, target):
        return pltpu.make_async_remote_copy(
            src_ref=src, dst_ref=dst, send_sem=sends.at[slot], recv_sem=recvs.at[slot],
            device_id=kinds[what][2](target), device_id_type=pl.DeviceIdType.MESH,
        )

    def start(what, key, scatter, src, dst):
        slot = slots[what, key, scatter] = len(slots)
        n, mine, _ = kinds[what]

        def body(k, carry):
            peer = lax.rem(mine + k, n)
            copy(src.at[peer if scatter else mine], dst.at[mine], what, slot, peer).start()
            return carry

        lax.fori_loop(1, n, body, 0)
        started.append((what, key, scatter, src, dst))

    def whole(what, key, scatter, src, dst):
        n, mine, _ = kinds[what]
        part = pl.ds(0, n - 1)
        return copy(
            src.at[part], dst.at[part], what, slots[what, key, scatter], lax.rem(mine + 1, n)
        )

    started = []

    for load in loads[:2]:
        load.wait()
    a = a_in[...]
    b = b_in[...]
    ag_a[0, col] = a.astype(BF16)
    ag_b[row] = b.astype(BF16)

    pl.semaphore_wait(barrier, n_row + n_col - 2)
    start("b", 0, False, ag_b, ag_b)
    start("a", 0, False, ag_a.at[0], ag_a.at[0])

    for load in loads[2:]:
        load.wait()
    for i, ref in enumerate((c_in, mc_in, vc_in)):
        for d in range(n_all):
            g, h = d // groups, d % groups
            split[i, d] = ref[g * chunk : (g + 1) * chunk, h * LANES : (h + 1) * LANES]
    st_a[0], st_a[1], st_a[2] = a, ma_in[...], va_in[...]
    st_b[0], st_b[1], st_b[2] = b, mb_in[...], vb_in[...]
    st_c[0], st_c[1], st_c[2] = split[0, me], split[1, me], split[2, me]
    c_b[...] = c_in[...].astype(BF16)
    load_x.wait()
    load_k.wait()

    pitch = x_f.shape[0] // tile_rows

    def widen(s, carry):
        for u in range(P_ROWS):
            i = s * P_ROWS + u
            x_f[pl.ds(pl.multiple_of(i * pitch, 8), depth), :] = x_s[i].astype(F32)
        return carry

    lax.fori_loop(0, tile_rows // P_ROWS, widen, 0)

    def turn(s, carry):
        for u in range(TURN):
            k = s * TURN + u
            x_t[k] = x_f[pl.ds(k, tile_rows, stride=pitch), :].astype(BF16)
        return carry

    lax.fori_loop(0, depth // TURN, turn, 0)

    steps = depth // DEEP
    per_step = n_all // steps
    mine_step = lax.div(me, per_step)

    def step_at(s):
        if steps & (steps - 1):
            return lax.rem(mine_step + 1 + s, steps)
        at = mine_step
        for bit in (1 << i for i in range(steps.bit_length() - 1)):
            if (steps - 1 - s) & bit:
                at = at + bit * (1 - 2 * lax.rem(lax.div(mine_step, bit), 2))
        return at

    def act(m, x):
        x = x.astype(F32)
        huber = jnp.clip(m - x, -1.0, 1.0)
        logit = 0.5 * jnp.tanh(0.5 * m) + jnp.where(x > 0, -0.5, 0.5)
        is_logit = jnp.broadcast_to(kind_s[0:1, :], m.shape) == 1
        return jnp.where(is_logit, logit, huber).astype(BF16)

    def product(p, b):
        return lax.dot_general(p, b, (((1,), (1,)), ((), ())), preferred_element_type=F32)

    spread = learn_rate * ITERS
    for it in range(ITERS):
        last = it == ITERS - 1
        counter = STEP + it + 1

        whole("a", it, False, ag_a.at[it], ag_a.at[it]).wait_recv()
        a_b[...] = ag_a[it].reshape(tile_rows, rank)
        a_f[...] = a_b[...].astype(F32)
        if it > 0:
            whole("c", it, False, ag_c.at[it], ag_c.at[it]).wait_recv()
            for d in range(n_all):
                g, h = d // groups, d % groups
                c_b[g * chunk : (g + 1) * chunk, h * LANES : (h + 1) * LANES] = ag_c[it, d]
        c_f[...] = c_b[...].astype(F32)

        def scale_rows(s, carry):
            at = pl.ds(pl.multiple_of(s * P_ROWS, P_ROWS), P_ROWS)
            wide = P_ROWS * tile_rows
            p = c_b[at, :][:, None, :] * a_b[...][None]
            p_s[pl.ds(pl.multiple_of(s * wide, wide), wide), :] = p.reshape(wide, rank)
            return carry

        lax.fori_loop(0, depth // P_ROWS, scale_rows, 0)

        if it == 0:
            whole("b", 0, False, ag_b, ag_b).wait_recv()
            b_f = ag_b[...].reshape(tile_cols, rank)
        else:
            for h in range(HALVES):
                whole("b", (it, h), False, ag_bh.at[it, h], ag_bh.at[it, h]).wait_recv()
            b_f = jnp.concatenate(
                [ag_bh[it, h].reshape(tile_cols, half) for h in range(HALVES)], axis=1
            )

        wide = DEEP * tile_rows

        def forward(g):
            span = pl.ds(pl.multiple_of(g * wide, wide), wide)
            x = x_t[pl.ds(pl.multiple_of(g * DEEP, DEEP), DEEP)].reshape(wide, tile_cols)
            y = act(product(p_s[span, :], b_f), x)
            y_s[span, :] = y
            return y

        slot = slots["c", it, True] = len(slots)
        started.append(("c", it, True, gs_c.at[it], rs_c.at[it]))
        later = forward(step_at(0))
        for s in range(steps):
            g = step_at(s)
            y = later
            if s < steps - 1:
                later = forward(step_at(s + 1))
            z = jnp.dot(y, b_f, preferred_element_type=F32).reshape(DEEP, tile_rows, rank)
            c_rows = c_f[pl.ds(pl.multiple_of(g * DEEP, DEEP), DEEP), :]
            part = jnp.sum(z * c_rows[:, None, :], axis=0)
            ga[...] = part if s == 0 else ga[...] + part
            part = (jnp.sum(z * a_f[...][None], axis=1) * scales[2]).astype(BF16)
            for q in range(per_step):
                u, h = q // groups, q % groups
                gs_c[it, g * per_step + q] = part[
                    u * chunk : (u + 1) * chunk, h * LANES : (h + 1) * LANES
                ]
            for t in range(steps // 2 + 1) if s == steps // 2 else range(steps // 2 + 1, steps) if s == steps - 1 else ():
                far = step_at(t)
                for q in range(per_step):
                    if t == steps - 1 and q == 0:
                        continue
                    peer = far * per_step + lax.rem(me - mine_step * per_step + q, per_step)
                    copy(gs_c.at[it, peer], rs_c.at[it, me], "c", slot, peer).start()

        rs_c[it, me] = gs_c[it, me]

        for h in range(HALVES):
            cut = slice(h * half, (h + 1) * half)
            g = lax.dot_general(
                y_s[...], p_s[:, cut], (((0,), (0,)), ((), ())), preferred_element_type=F32
            ) * scales[1]
            gb[:, cut] = g
            gs_b[it, h] = g.astype(BF16).reshape(n_row, own_b, half)
            start("b", (it, h), True, gs_b.at[it, h], rs_b.at[it, h])

        ga[...] = ga[...] * scales[0]
        gs_a[it] = ga[...].astype(BF16).reshape(n_col, own_a, rank)
        start("a", it, True, gs_a.at[it], rs_a.at[it])

        whole("c", it, True, gs_c.at[it], rs_c.at[it]).wait_recv()
        st_c[0], st_c[1], st_c[2] = adam_step(
            st_c[0], st_c[1], st_c[2], jnp.sum(rs_c[it].astype(F32), axis=0), counter
        )
        c = (split[0, me] - st_c[0]) / spread if last else st_c[0]
        ag_c[it + 1, me] = c.astype(BF16)
        land = oc if last else ag_c.at[it + 1]
        start("c", it + 1, False, ag_c.at[it + 1], land)
        if last:
            put_c = pltpu.make_async_copy(ag_c.at[it + 1, me], oc.at[me], out_sem.at[2])
            put_c.start()

        whole("a", it, True, gs_a.at[it], rs_a.at[it]).wait_recv()
        grad = ga[pl.ds(pl.multiple_of(col * own_a, own_a), own_a), :]
        for k in range(1, n_col):
            grad = grad + rs_a[it, lax.rem(col + k, n_col)].astype(F32)
        st_a[0], st_a[1], st_a[2] = adam_step(st_a[0], st_a[1], st_a[2], grad, counter)
        if last:
            out_a[...] = (a_in[...] - st_a[0]) / spread
            put_a = pltpu.make_async_copy(out_a, oa, out_sem.at[0])
            put_a.start()
        else:
            ag_a[it + 1, col] = st_a[0].astype(BF16)
            start("a", it + 1, False, ag_a.at[it + 1], ag_a.at[it + 1])

        for h in range(HALVES):
            cut = slice(h * half, (h + 1) * half)
            whole("b", (it, h), True, gs_b.at[it, h], rs_b.at[it, h]).wait_recv()
            grad = gb[pl.ds(pl.multiple_of(row * own_b, own_b), own_b), cut]
            for k in range(1, n_row):
                grad = grad + rs_b[it, h, lax.rem(row + k, n_row)].astype(F32)
            f, m, v = adam_step(st_b[0, :, cut], st_b[1, :, cut], st_b[2, :, cut], grad, counter)
            if last:
                out_b[:, cut] = (b_in[:, cut] - f) / spread
            else:
                st_b[0, :, cut], st_b[1, :, cut], st_b[2, :, cut] = f, m, v
                ag_bh[it + 1, h, row] = f.astype(BF16)
                start("b", (it + 1, h), False, ag_bh.at[it + 1, h], ag_bh.at[it + 1, h])
        if last:
            put_b = pltpu.make_async_copy(out_b, ob, out_sem.at[1])
            put_b.start()

    whole("c", ITERS, False, ag_c.at[ITERS], oc).wait_recv()
    for args in started:
        whole(*args).wait_send()
    for put in (put_a, put_b, put_c):
        put.wait()


def hand_on(a, b, c, oa, ob, oc):
    oa[...] = a[...]
    ob[...] = b[...]
    chunk = c.shape[1]
    groups = oc.shape[1] // LANES
    for d in range(c.shape[0]):
        g, h = d // groups, d % groups
        oc[g * chunk : (g + 1) * chunk, h * LANES : (h + 1) * LANES] = c[d].astype(F32)


def shards(tensor, loss_kind, a, b, c, ma, va, mb, vb, mc, vc):
    tile_rows, depth, tile_cols = tensor.shape
    rank = a.shape[1]
    half = rank // HALVES
    n_row = lax.axis_size("row")
    n_col = lax.axis_size("col")
    n_all = n_row * n_col
    full_rows = tile_rows * n_row
    full_cols = tile_cols * n_col
    scales = (
        1.0 / math.sqrt(full_cols * depth),
        1.0 / math.sqrt(full_rows * depth),
        1.0 / math.sqrt(full_rows * full_cols),
    )
    chunk = depth * rank // (n_all * LANES)
    own_a, own_b = a.shape[0], b.shape[0]
    hbm = pl.BlockSpec(memory_space=pl.ANY)
    slots = ITERS * (4 + 2 * HALVES) + 2
    outs = pl.pallas_call(
        functools.partial(kernel, n_row, n_col, scales),
        out_shape=(
            jax.ShapeDtypeStruct(a.shape, F32),
            jax.ShapeDtypeStruct(b.shape, F32),
            jax.ShapeDtypeStruct((n_all, chunk, LANES), BF16),
        ),
        in_specs=[hbm] * 11,
        out_specs=[hbm] * 3,
        scratch_shapes=[
            pltpu.VMEM(tensor.shape, tensor.dtype),
            pltpu.VMEM((tile_rows * (depth + PAD) + depth, tile_cols), F32),
            pltpu.VMEM((depth, tile_rows, tile_cols), tensor.dtype),
            pltpu.VMEM((8, tile_cols), jnp.int32),
            pltpu.VMEM((ITERS, n_col, own_a, rank), BF16),
            pltpu.VMEM((n_row, own_b, rank), BF16),
            pltpu.VMEM((ITERS, HALVES, n_row, own_b, half), BF16),
            pltpu.VMEM((ITERS + 1, n_all, chunk, LANES), BF16),
            pltpu.VMEM((ITERS, n_col, own_a, rank), BF16),
            pltpu.VMEM((ITERS, HALVES, n_row, own_b, half), BF16),
            pltpu.VMEM((ITERS, n_all, chunk, LANES), BF16),
            pltpu.VMEM((ITERS, n_col, own_a, rank), BF16),
            pltpu.VMEM((ITERS, HALVES, n_row, own_b, half), BF16),
            pltpu.VMEM((ITERS, n_all, chunk, LANES), BF16),
            pltpu.VMEM((tile_rows, rank), BF16),
            pltpu.VMEM((tile_rows, rank), F32),
            pltpu.VMEM((depth, rank), BF16),
            pltpu.VMEM((depth, rank), F32),
            pltpu.VMEM((tile_rows, rank), F32),
            pltpu.VMEM((tile_cols, rank), F32),
            pltpu.VMEM((3, own_a, rank), F32),
            pltpu.VMEM((3, own_b, rank), F32),
            pltpu.VMEM((3, chunk, LANES), F32),
            pltpu.VMEM((3, n_all, chunk, LANES), F32),
            pltpu.VMEM((tile_rows * depth, rank), BF16),
            pltpu.VMEM((tile_rows * depth, tile_cols), BF16),
            *[pltpu.VMEM(f.shape, F32) for f in (a, b)],
            *[pltpu.VMEM(f.shape, F32) for f in (a, b, c, ma, va, mb, vb, mc, vc)],
            pltpu.SemaphoreType.DMA((11,)),
            pltpu.SemaphoreType.DMA((slots,)),
            pltpu.SemaphoreType.DMA((slots,)),
            pltpu.SemaphoreType.DMA((3,)),
        ],
        compiler_params=pltpu.CompilerParams(
            collective_id=0, has_side_effects=True, vmem_limit_bytes=60 * 1024 * 1024
        ),
    )(tensor, loss_kind, a, b, c, ma, va, mb, vb, mc, vc)
    vmem = pl.BlockSpec(memory_space=pltpu.VMEM)
    return pl.pallas_call(
        hand_on,
        out_shape=tuple(jax.ShapeDtypeStruct(f.shape, F32) for f in (a, b, c)),
        in_specs=[vmem] * 3,
        out_specs=[vmem] * 3,
    )(*outs)


def solution(mesh):
    in_specs = (
        P("row", None, "col"),
        P("row", None, "col"),
        P(("row", "col"), None),
        P(("col", "row"), None),
        P(),
        P(("row", "col"), None),
        P(("row", "col"), None),
        P(("col", "row"), None),
        P(("col", "row"), None),
        P(),
        P(),
    )
    out_specs = (P(("row", "col"), None), P(("col", "row"), None), P())
    return jax.shard_map(shards, mesh=mesh, in_specs=in_specs, out_specs=out_specs, check_vma=False)
```
